32 devices in a mesh: ctx: 16 (over z, y, x), head: 2 (over core).
Axes of the slice: x: 2, y: 2, z: 4, core: 2. Of those that a mesh axis runs over, the one named last changes fastest.
Arguments:
- tokens: bfloat16 [4096, 3072], P('ctx'), may hold values from -6 to 6
- w_query: bfloat16 [3072, 4096], P('ctx', 'head'), may hold values from -0.109375 to 0.109375
- w_key: bfloat16 [3072, 4096], P('ctx', 'head'), may hold values from -0.109375 to 0.109375
- w_value: bfloat16 [3072, 4096], P('ctx', 'head'), may hold values from -0.109375 to 0.109375
- log_decay: float32 [32, 4096], P('head', 'ctx'), may hold values from -1 to 0
- norm_gain: float32 [4096], P('head'), may hold values from 0.25 to 1.75
- w_out: bfloat16 [4096, 3072], P('head', 'ctx'), may hold values from -0.09375 to 0.09375
Outputs:
- layer_out: bfloat16 [4096, 3072], P('ctx', 'head')
The draws below stay inside these ranges and needn't reach their ends.
All inputs are finite; a program needn't handle non-finite values.
Results may differ from the reference program's by a relative error of at most 0.014.
Values may be sent and summed in bfloat16 or wider, within the bound.
No kernel may reach another device: no remote copies, remote signals or barrier semaphores. Data moves between devices by JAX's collectives and lax.ppermute only.
A program may use at most 128 MiB of HBM per device.

```python
import math
import jax
import jax.numpy as jnp
from jax import lax

D = 3072
HEADS = 32
DH = 128
TOK_DEV = 256
SEQ = 4096
HD = 4096


def draw_log_decay(key, part):
    keys_all = jax.random.split(jax.random.fold_in(key, 7), 7)
    fast_count = HEADS // 2
    order = jax.random.permutation(keys_all[0], HEADS)
    fast = order < fast_count
    quick_decay_rate = jnp.exp(jax.random.uniform(keys_all[1], (HEADS,), jnp.float32, math.log(1.0 / 50.0), math.log(1.0 / 30.0)))
    slow_rate = jnp.exp(jax.random.uniform(keys_all[2], (HEADS,), jnp.float32, math.log(0.05 / SEQ), math.log(0.2 / SEQ)))
    rate = jnp.where(fast, quick_decay_rate, slow_rate)
    factor = jnp.exp(jax.random.uniform(keys_all[3], (HEADS, SEQ // TOK_DEV), jnp.float32, math.log(0.5), math.log(2.0)))
    factor = jnp.repeat(factor, TOK_DEV, axis=1)
    jitter = jax.random.uniform(keys_all[4], (HEADS, SEQ), jnp.float32, 0.5, 1.5)
    initial_shift = -rate[:, None] * factor * jitter
    spots = jax.random.randint(keys_all[5], (HEADS, 2), 0, SEQ)
    recursion_depth_count = jax.random.uniform(keys_all[6], (HEADS, 2), jnp.float32, math.log(0.5), math.log(0.8))
    sequence_indices = jnp.arange(SEQ)[None, None, :] == spots[:, :, None]
    segment_element_length = jnp.sum(jnp.where(sequence_indices, recursion_depth_count[:, :, None], 0.0), axis=1)
    return (initial_shift + segment_element_length).astype(jnp.float32)


def levels(own_key, shape, cuts, least, largest):
    def one(dim, parts):
        steps = jax.random.uniform(jax.random.fold_in(jax.random.fold_in(own_key, 6), dim), (parts,), jnp.float32, least / len(cuts), largest / len(cuts))
        return jnp.repeat(jnp.exp(steps), shape[dim] // parts).reshape((-1,) + (1,) * (len(shape) - dim - 1))

    level = one(*cuts[0])
    for cut in cuts[1:]:
        level = level * one(*cut)
    return level


def noise(key, dims, scale, reach, cuts=(), dtype=jnp.bfloat16):
    level = levels(key, dims, cuts, -0.22, 0.18) if cuts else 1.0
    result = jax.random.normal(key, dims, jnp.float32) * scale * level
    return jnp.minimum(jnp.maximum(result, -reach), reach).astype(dtype)


def setup_inputs(seed: int = 0) -> dict:
    seeds = jax.random.split(jax.random.key(seed), 8)
    tokens = noise(seeds[0], (SEQ, D), 1.0, 6.0, ((0, 16),))
    w_query = noise(seeds[1], (D, HD), D ** -0.5, 0.109375, ((0, 16), (1, 2)))
    w_key = noise(seeds[2], (D, HD), D ** -0.5, 0.109375, ((0, 16), (1, 2)))
    w_value = noise(seeds[3], (D, HD), D ** -0.5, 0.109375, ((0, 16), (1, 2)))
    log_decay = draw_log_decay(jax.random.fold_in(seeds[7], 71), 0)
    norm_gain = jnp.clip(1.0 + 0.15 * jax.random.normal(seeds[5], (HD,), jnp.float32), 0.25, 1.75)
    w_out = noise(seeds[6], (HD, D), HD ** -0.5, 0.09375, ((0, 2), (1, 16)))
    return dict(tokens=tokens, w_query=w_query, w_key=w_key, w_value=w_value, log_decay=log_decay, norm_gain=norm_gain, w_out=w_out)


def reference(tokens, w_query, w_key, w_value, log_decay, norm_gain, w_out):
    blocks = SEQ // TOK_DEV
    causal = jnp.arange(TOK_DEV)[:, None] >= jnp.arange(TOK_DEV)[None, :]
    gain = norm_gain.reshape(HEADS, DH)

    def one_block(state, inputs):
        rows_in, decay_rows = inputs
        queries = jax.nn.silu(jnp.dot(rows_in, w_query, preferred_element_type=jnp.float32)).astype(jnp.bfloat16)
        keys = jax.nn.silu(jnp.dot(rows_in, w_key, preferred_element_type=jnp.float32)).astype(jnp.bfloat16)
        values = jnp.dot(rows_in, w_value, preferred_element_type=jnp.float32).astype(jnp.bfloat16)
        queries = queries.reshape(TOK_DEV, HEADS, DH).astype(jnp.float32)
        keys = keys.reshape(TOK_DEV, HEADS, DH).astype(jnp.float32)
        values = values.reshape(TOK_DEV, HEADS, DH).astype(jnp.float32)
        cumul = jnp.cumsum(decay_rows, axis=1)
        keep = jnp.exp(cumul[:, -1:] - cumul).T
        decayed = (keys * keep[:, :, None]).astype(jnp.bfloat16).astype(jnp.float32)
        block_state = jnp.einsum('thd,the->hde', decayed, values, precision=lax.Precision.HIGHEST)
        diff = cumul[:, :, None] - cumul[:, None, :]
        decay = jnp.where(causal[None], jnp.exp(jnp.where(causal[None], diff, 0.0)), 0.0)
        scores = jnp.einsum('thd,shd->hts', queries, keys, precision=lax.Precision.HIGHEST) * decay
        weight_tensors = scores.astype(jnp.bfloat16).astype(jnp.float32)
        intra = jnp.einsum('hts,shd->thd', weight_tensors, values, precision=lax.Precision.HIGHEST)
        scaled = queries * jnp.exp(cumul).T[:, :, None]
        inter = jnp.einsum('thd,hde->the', scaled, state, precision=lax.Precision.HIGHEST)
        mixed = intra + inter
        normed = mixed * lax.rsqrt(lax.optimization_barrier(jnp.mean(mixed * mixed, axis=-1, keepdims=True)) + 1e-06) * gain
        normed = normed.astype(jnp.bfloat16).reshape(TOK_DEV, HD)
        block_out = jnp.dot(normed, w_out, preferred_element_type=jnp.float32).astype(jnp.bfloat16)
        new_state = jnp.exp(cumul[:, -1])[:, None, None] * state + block_state
        return (new_state, block_out)
    inputs = (tokens.reshape(blocks, TOK_DEV, D), log_decay.reshape(HEADS, blocks, TOK_DEV).transpose(1, 0, 2))
    start = jnp.zeros((HEADS, DH, DH), jnp.float32)
    final_state, result_list = lax.scan(one_block, start, inputs)
    return result_list.reshape(SEQ, D)
```

```python
import functools
import math

import jax
import jax.numpy as jnp
from jax import lax
from jax.experimental import pallas as pl
from jax.experimental.pallas import tpu as pltpu
from jax.sharding import PartitionSpec as P

F32 = jnp.float32
BF16 = jnp.bfloat16


def tie(value, *earlier):
    return lax.optimization_barrier((value, *earlier))[0]


def state_body(pos, k_ref, v_ref, cum_t_ref, ent_ref, total_ref, *, heads, head_dim):
    @pl.when(pl.program_id(0) == 0)
    def _():
        total_ref[...] = jnp.zeros_like(total_ref)

    ent_ref[0] = total_ref[...]
    rows = k_ref.shape[1]
    for i in range(heads):
        cols = slice(i * head_dim, (i + 1) * head_dim)
        cum = cum_t_ref[0, :, i : i + 1]
        last = cum_t_ref[0, rows - 1 : rows, i : i + 1]
        decayed = (k_ref[0, :, cols].astype(F32) * jnp.exp(last - cum)).astype(BF16)
        block = lax.dot_general(
            decayed, v_ref[0, :, cols], (((0,), (0,)), ((), ())), preferred_element_type=F32
        )
        total_ref[i] = jnp.exp(last) * total_ref[i] + block


def mix_body(
    pos, q_ref, k_ref, v_ref, cum_ref, cum_t_ref, before_ref, ent_ref, group_ref, gain_ref, out_ref,
    *, heads, head_dim,
):
    rows = q_ref.shape[1]
    causal = lax.broadcasted_iota(jnp.int32, (rows, rows), 0) >= lax.broadcasted_iota(
        jnp.int32, (rows, rows), 1
    )
    for i in range(heads):
        cols = slice(i * head_dim, (i + 1) * head_dim)
        q, k, v = q_ref[0, :, cols], k_ref[0, :, cols], v_ref[0, :, cols]
        cum = cum_t_ref[0, :, i : i + 1]
        diff = cum - cum_ref[0, i : i + 1, :]
        decay = jnp.where(causal, jnp.exp(jnp.where(causal, diff, 0.0)), 0.0)
        scores = lax.dot_general(q, k, (((1,), (1,)), ((), ())), preferred_element_type=F32)
        weights = (scores * decay).astype(BF16)
        intra = jnp.dot(weights, v, preferred_element_type=F32)
        state = ent_ref[0, i] + jnp.exp(before_ref[0, :, i : i + 1]) * group_ref[i]
        high = state.astype(BF16)
        low = (state - high.astype(F32)).astype(BF16)
        inter = jnp.dot(q, high, preferred_element_type=F32) + jnp.dot(
            q, low, preferred_element_type=F32
        )
        mixed = intra + jnp.exp(cum) * inter
        scale = lax.rsqrt(jnp.mean(mixed * mixed, axis=-1, keepdims=True) + 1e-06)
        out_ref[0, :, cols] = (mixed * scale * gain_ref[:, cols]).astype(BF16)


def block_states(pos, k, v, cum_t, heads, head_dim):
    count, rows, width = k.shape
    at = lambda b, p: (p[b], 0, 0)
    return pl.pallas_call(
        functools.partial(state_body, heads=heads, head_dim=head_dim),
        grid_spec=pltpu.PrefetchScalarGridSpec(
            num_scalar_prefetch=1,
            grid=(count,),
            in_specs=[
                pl.BlockSpec((1, rows, width), at),
                pl.BlockSpec((1, rows, width), at),
                pl.BlockSpec((1, rows, heads), lambda b, p: (b, 0, 0)),
            ],
            out_specs=[
                pl.BlockSpec((1, heads, head_dim, head_dim), lambda b, p: (b, 0, 0, 0)),
                pl.BlockSpec((heads, head_dim, head_dim), lambda b, p: (0, 0, 0)),
            ],
        ),
        out_shape=[
            jax.ShapeDtypeStruct((count, heads, head_dim, head_dim), F32),
            jax.ShapeDtypeStruct((heads, head_dim, head_dim), F32),
        ],
        name="block_states",
    )(pos, k, v, cum_t)


def mix(pos, q, k, v, cum, cum_t, before, ent, group, gain, heads, head_dim):
    count, rows, width = k.shape
    at = lambda b, p: (p[b], 0, 0)
    plain = lambda b, p: (b, 0, 0)
    return pl.pallas_call(
        functools.partial(mix_body, heads=heads, head_dim=head_dim),
        grid_spec=pltpu.PrefetchScalarGridSpec(
            num_scalar_prefetch=1,
            grid=(count,),
            in_specs=[
                pl.BlockSpec((1, rows, width), at),
                pl.BlockSpec((1, rows, width), at),
                pl.BlockSpec((1, rows, width), at),
                pl.BlockSpec((1, heads, rows), plain),
                pl.BlockSpec((1, rows, heads), plain),
                pl.BlockSpec((1, 1, heads), plain),
                pl.BlockSpec((1, heads, head_dim, head_dim), lambda b, p: (b, 0, 0, 0)),
                pl.BlockSpec((heads, head_dim, head_dim), lambda b, p: (0, 0, 0)),
                pl.BlockSpec((1, width), lambda b, p: (0, 0)),
            ],
            out_specs=pl.BlockSpec((1, rows, width), at),
        ),
        out_shape=jax.ShapeDtypeStruct((count, rows, width), BF16),
        name="mix",
    )(pos, q, k, v, cum, cum_t, before, ent, group, gain)


def per_device(tokens, w_query, w_key, w_value, log_decay, norm_gain, w_out, *, n, nh):
    rows, model = tokens.shape
    heads_here = log_decay.shape[0]
    head_dim = w_query.shape[1] // heads_here
    g = math.gcd(heads_here, max(n // 2, 1))
    ng = n // g
    heads = heads_here // g
    width = heads * head_dim
    c = lax.axis_index("ctx")
    h = lax.axis_index("head")
    member = c % g
    group = c // g
    groups = [[a * g + b for b in range(g)] for a in range(ng)]
    bits = [1 << i for i in range(g.bit_length() - 1)][::-1]
    orders = (bits[:1] + bits[1:][::-1], bits)

    def exchange(value, where):
        pairs = []
        for a in range(n):
            for b in range(nh):
                to = where(a, b)
                if to is not None:
                    pairs.append((a * nh + b, to[0] * nh + to[1]))
        return lax.ppermute(value, ("ctx", "head"), pairs)

    def spread(value, split, concat):
        return lax.all_to_all(
            value, "ctx", split, concat, axis_index_groups=groups, tiled=True
        )

    def over_groups(piece):
        pieces = [piece]
        step = 1
        while step < ng:
            got = [exchange(p, lambda a, b: (a ^ (step * g), b)) for p in pieces]
            pieces += got
            step *= 2
        return pieces

    def true_order(pieces, index):
        if len(pieces) == 1:
            return pieces
        half = len(pieces) // 2
        low, high = true_order(pieces[:half], index), true_order(pieces[half:], index)
        upper = (index & half) != 0
        return [jnp.where(upper, b, a) for a, b in zip(low, high)] + [
            jnp.where(upper, a, b) for a, b in zip(low, high)
        ]

    key_here = spread(w_key, 1, 0)
    cumul = jnp.cumsum(log_decay, axis=1).reshape(g, heads * rows)
    cumul = spread(tie(cumul, key_here), 0, 0).reshape(g, heads, rows)
    value_here = spread(tie(w_value, key_here), 1, 0)

    share = model // nh
    own = lax.dynamic_slice_in_dim(tie(tokens, key_here), h * share, share, axis=1)
    gathered = own[None]
    for stage in range(len(bits)):
        got = exchange(gathered, lambda a, b: (a ^ orders[b & 1][stage], b))
        gathered = jnp.concatenate([gathered, got], axis=0)
    query_here = spread(tie(w_query, value_here), 1, 0)
    out_here = spread(tie(w_out, query_here).reshape(g, width, -1), 0, 0)

    axes = orders[0][::-1]
    swap = [orders[1][::-1].index(b) for b in axes]
    shares = [gathered]
    step = 1
    while step < nh:
        shares += [exchange(s, lambda a, b: (a, b ^ step)) for s in shares]
        step *= 2

    def canonical(value, parity):
        cube = value.reshape((2,) * len(bits) + value.shape[1:])
        tail = tuple(range(len(bits), cube.ndim))
        other = cube.transpose(tuple(swap) + tail).reshape(value.shape)
        return jnp.where(parity == 1, other, value)

    shares = [canonical(s, (h ^ p) & 1) for p, s in enumerate(shares)]
    shares = [s.reshape(g * rows, share) for s in shares]

    if nh == ng:
        aligned = true_order(shares, h ^ group)

        def project(here):
            pieces = over_groups(here)
            return sum(
                jnp.dot(t, w, preferred_element_type=F32) for t, w in zip(aligned, pieces)
            )
    else:
        full = jnp.concatenate(true_order(shares, h), axis=1)

        def project(here):
            weight = jnp.concatenate(true_order(over_groups(here), group), axis=0)
            return jnp.dot(full, weight, preferred_element_type=F32)

    def shaped(raw):
        return raw.astype(BF16).reshape(g, rows, width)

    keys = shaped(jax.nn.silu(project(key_here)))
    values = shaped(project(value_here))

    apart = jnp.arange(g, dtype=jnp.int32) ^ member.astype(jnp.int32)
    pos = jnp.zeros_like(apart)
    for place, bit in enumerate(axes[::-1]):
        pos = pos + jnp.where((apart & bit) != 0, 1 << place, 0)
    cum_t = cumul.transpose(0, 2, 1)
    last = cumul[:, :, -1]
    through = jnp.cumsum(last, axis=0)
    before = through - last
    ent, total = block_states(pos, keys, values, cum_t, heads, head_dim)

    keep = jnp.exp(through[-1])
    later = lambda by: (lambda a, b: (a + by * g, b) if a + by * g < n else None)
    entering = exchange(total, later(1))
    step = 1
    if ng > 2:
        keep = exchange(keep, later(1))
    while step < ng - 1:
        entering = entering + keep[:, None, None] * exchange(entering, later(step))
        keep = keep * exchange(keep, later(step))
        step *= 2

    queries = shaped(jax.nn.silu(project(query_here)))
    gain = lax.dynamic_slice_in_dim(norm_gain, member * width, width)[None]
    normed = mix(
        pos, queries, keys, values, cumul, cum_t, before[:, None, :], ent, entering, gain,
        heads, head_dim,
    )

    out_cols = model // nh
    local = out_here.transpose(1, 0, 2).reshape(width, -1)
    pieces = true_order(over_groups(local), group)
    merged = len(pieces) // nh if len(pieces) >= nh else 0
    if merged == 1:
        stacked = jnp.stack(pieces)
    else:
        stacked = jnp.concatenate(pieces, axis=1).reshape(width, nh, out_cols).transpose(1, 0, 2)
    normed = normed.reshape(g * rows, width)
    partial = 0.0
    for apart_by in range(nh):
        part_w = lax.dynamic_index_in_dim(stacked, h ^ apart_by, 0, False)
        part_n = normed
        if apart_by:
            part_w = exchange(part_w, lambda a, b: (a, b ^ apart_by))
            part_n = exchange(part_n, lambda a, b: (a, b ^ apart_by))
        partial = partial + jnp.dot(part_n, part_w, preferred_element_type=F32)
    partial = partial.astype(BF16)

    chunks = max(len(bits), 1)
    span = out_cols // chunks
    summed = []
    for i in range(chunks):
        cols = slice(i * span, (i + 1) * span if i + 1 < chunks else out_cols)
        piece = partial[:, cols].reshape((2,) * len(bits) + (rows, -1))
        left = list(axes)
        for bit in bits[i:] + bits[:i]:
            axis = left.index(bit)
            left.pop(axis)
            kept = lax.index_in_dim(piece, 0, axis, False)
            sent = lax.index_in_dim(piece, 1, axis, False)
            got = exchange(sent, lambda a, b: (a ^ bit, b))
            piece = (kept.astype(F32) + got.astype(F32)).astype(BF16)
        summed.append(piece)
    return jnp.concatenate(summed, axis=1)


def solution(mesh):
    placed = (
        P("ctx", None),
        P("ctx", "head"),
        P("ctx", "head"),
        P("ctx", "head"),
        P("head", "ctx"),
        P("head"),
        P("head", "ctx"),
    )
    body = functools.partial(per_device, n=mesh.shape["ctx"], nh=mesh.shape["head"])
    return jax.shard_map(
        body, mesh=mesh, in_specs=placed, out_specs=P("ctx", "head"), check_vma=False
    )
```

```python
import functools
import math

import jax
import jax.numpy as jnp
from jax import lax
from jax.experimental import pallas as pl
from jax.experimental.pallas import tpu as pltpu
from jax.sharding import PartitionSpec as P


F32 = jnp.float32
BF16 = jnp.bfloat16


def silu(x):
    return x / (1.0 + jnp.exp(-x))


def block_state(k, v, cum_t, heads, head_dim):
    rows = k.shape[0]
    out = []
    for i in range(heads):
        cols = slice(i * head_dim, (i + 1) * head_dim)
        cum = cum_t[:, i : i + 1]
        last = cum_t[rows - 1 : rows, i : i + 1]
        decayed = (k[:, cols].astype(F32) * jnp.exp(last - cum)).astype(BF16)
        out.append(
            lax.dot_general(
                decayed, v[:, cols], (((0,), (0,)), ((), ())), preferred_element_type=F32
            )
        )
    return out


def state_body(where, k_ref, v_ref, cum_t_ref, out_ref, *, heads, head_dim):
    for i, s in enumerate(block_state(k_ref[0], v_ref[0], cum_t_ref[0], heads, head_dim)):
        out_ref[0, i] = s


def block_states(block_at, k, v, cum_t, heads, head_dim):
    count, rows, width = k.shape
    here = lambda i, w: (i, 0, 0)
    return pl.pallas_call(
        functools.partial(state_body, heads=heads, head_dim=head_dim),
        grid_spec=pltpu.PrefetchScalarGridSpec(
            num_scalar_prefetch=1,
            grid=(count,),
            in_specs=[
                pl.BlockSpec((1, rows, width), here),
                pl.BlockSpec((1, rows, width), here),
                pl.BlockSpec((1, rows, heads), lambda i, w: (w[i], 0, 0)),
            ],
            out_specs=pl.BlockSpec(
                (1, heads, head_dim, head_dim), lambda i, w: (i, 0, 0, 0)
            ),
        ),
        out_shape=jax.ShapeDtypeStruct((count, heads, head_dim, head_dim), F32),
        name="block_states",
    )(block_at, k, v, cum_t)


def halves(step, refs):
    pair, got, pair_other, got_other = refs
    own = lambda: jnp.where(step < 2, pair[0], got[0])
    other = lambda: jnp.where(step % 2 == 0, pair_other[0], got_other[0])
    return own, other


def family_specs(rows, share):
    return [
        pl.BlockSpec((1, rows, share), lambda i, w: (jnp.minimum(i, 1), 0, 0)),
        pl.BlockSpec((1, rows, share), lambda i, w: (jnp.maximum(i - 2, 0), 0, 0)),
        pl.BlockSpec((1, rows, share), lambda i, w: (i // 2, 0, 0)),
        pl.BlockSpec((1, rows, share), lambda i, w: (i // 2, 0, 0)),
    ]


def product(tokens, weight_ref, first, second):
    cut = weight_ref.shape[1]
    return jnp.dot(
        tokens[:, :cut], weight_ref[first], preferred_element_type=F32
    ) + jnp.dot(tokens[:, cut:], weight_ref[second], preferred_element_type=F32)


def keys_values_body(
    where, pair, got, pair_other, got_other, wk_ref, wv_ref, cum_t_ref, k_ref, v_ref, state_ref,
    *, heads, head_dim,
):
    own, other = (x() for x in halves(pl.program_id(0), (pair, got, pair_other, got_other)))
    mine, swap = where[4], where[5]
    at = lambda side, i: 2 * side + (i ^ swap)
    full = lambda w: product(own, w, at(mine, 0), at(mine, 1)) + product(
        other, w, at(1 - mine, 0), at(1 - mine, 1)
    )
    k = silu(full(wk_ref)).astype(BF16)
    v = full(wv_ref).astype(BF16)
    k_ref[0] = k
    v_ref[0] = v
    for i, s in enumerate(block_state(k, v, cum_t_ref[0], heads, head_dim)):
        state_ref[0, i] = s


def keys_values(table, family, wk, wv, cum_t, heads, head_dim):
    _, rows, share = family[0].shape
    width = wk.shape[2]
    whole = lambda i, w: (0, 0, 0)
    here = lambda i, w: (i, 0, 0)
    return pl.pallas_call(
        functools.partial(keys_values_body, heads=heads, head_dim=head_dim),
        grid_spec=pltpu.PrefetchScalarGridSpec(
            num_scalar_prefetch=1,
            grid=(4,),
            in_specs=family_specs(rows, share)
            + [
                pl.BlockSpec(wk.shape, whole),
                pl.BlockSpec(wv.shape, whole),
                pl.BlockSpec((1, rows, heads), lambda i, w: (w[i], 0, 0)),
            ],
            out_specs=[
                pl.BlockSpec((1, rows, width), here),
                pl.BlockSpec((1, rows, width), here),
                pl.BlockSpec((1, heads, head_dim, head_dim), lambda i, w: (i, 0, 0, 0)),
            ],
        ),
        out_shape=[
            jax.ShapeDtypeStruct((4, rows, width), BF16),
            jax.ShapeDtypeStruct((4, rows, width), BF16),
            jax.ShapeDtypeStruct((4, heads, head_dim, head_dim), F32),
        ],
    )(table, *family, wk, wv, cum_t)


def query_body(where, *refs, late):
    tokens, (w_ref, *rest) = refs[:8], refs[8:]
    step = pl.program_id(0)
    mine, swap = where[0], where[1]
    use_own = (mine == 1) if late else (mine == 0)
    for f in range(2):
        own, other = halves(step % 4, tokens[4 * f : 4 * f + 4])

        @pl.when(step // 4 == f)
        def _():
            for flag, side in ((use_own, own), (jnp.logical_not(use_own), other)):

                @pl.when(flag)
                def _():
                    part = product(side(), w_ref, swap, 1 ^ swap)
                    if late:
                        rest[1][0] = silu(rest[0][0] + part).astype(BF16)
                    else:
                        rest[0][0] = part


def query_part(table, near, far, weight, early):
    _, rows, share = near[0].shape
    width = weight.shape[2]
    late = early is not None
    here = lambda i, w: (i, 0, 0)

    def moved(spec, f):
        inner = spec.index_map
        return pl.BlockSpec(
            spec.block_shape,
            (lambda i, w: inner(jnp.minimum(i, 3), w)) if f == 0 else (
                lambda i, w: inner(jnp.maximum(i - 4, 0), w)
            ),
        )

    specs = [moved(s, f) for f in range(2) for s in family_specs(rows, share)]
    specs.append(pl.BlockSpec(weight.shape, lambda i, w: (0, 0, 0)))
    args = [*near, *far, weight]
    if late:
        specs.append(pl.BlockSpec((1, rows, width), here))
        args.append(early)
    return pl.pallas_call(
        functools.partial(query_body, late=late),
        grid_spec=pltpu.PrefetchScalarGridSpec(
            num_scalar_prefetch=1,
            grid=(8,),
            in_specs=specs,
            out_specs=pl.BlockSpec((1, rows, width), here),
        ),
        out_shape=jax.ShapeDtypeStruct((8, rows, width), BF16 if late else F32),
    )(table, *args)


def mix_body(
    pos, q_ref, k_ref, v_ref, cum_ref, cum_t_ref, state_ref, group_ref, gain_ref, out_ref, carry_ref,
    *, heads, head_dim,
):
    @pl.when(pl.program_id(0) == 0)
    def _():
        carry_ref[...] = group_ref[...]

    rows = q_ref.shape[1]
    causal = lax.broadcasted_iota(jnp.int32, (rows, rows), 0) >= lax.broadcasted_iota(
        jnp.int32, (rows, rows), 1
    )
    for i in range(heads):
        cols = slice(i * head_dim, (i + 1) * head_dim)
        q, k, v = q_ref[0, :, cols], k_ref[0, :, cols], v_ref[0, :, cols]
        cum = cum_t_ref[0, :, i : i + 1]
        last = cum_t_ref[0, rows - 1 : rows, i : i + 1]
        diff = cum - cum_ref[0, i : i + 1, :]
        decay = jnp.where(causal, jnp.exp(jnp.where(causal, diff, 0.0)), 0.0)
        scores = lax.dot_general(q, k, (((1,), (1,)), ((), ())), preferred_element_type=F32)
        weights = (scores * decay).astype(BF16)
        intra = jnp.dot(weights, v, preferred_element_type=F32)
        state = carry_ref[i]
        carry_ref[i] = jnp.exp(last) * state + state_ref[0, i]
        high = state.astype(BF16)
        low = (state - high.astype(F32)).astype(BF16)
        inter = jnp.dot(q, high, preferred_element_type=F32) + jnp.dot(
            q, low, preferred_element_type=F32
        )
        mixed = intra + jnp.exp(cum) * inter
        scale = lax.rsqrt(jnp.mean(mixed * mixed, axis=-1, keepdims=True) + 1e-06)
        out_ref[0, :, cols] = (mixed * scale * gain_ref[:, cols]).astype(BF16)


def mix(pos, q, k, v, cum, cum_t, states, group, gain, heads, head_dim):
    count, rows, width = k.shape
    at = lambda b, p: (p[b], 0, 0)
    plain = lambda b, p: (b, 0, 0)
    return pl.pallas_call(
        functools.partial(mix_body, heads=heads, head_dim=head_dim),
        grid_spec=pltpu.PrefetchScalarGridSpec(
            num_scalar_prefetch=1,
            grid=(count,),
            in_specs=[
                pl.BlockSpec((1, rows, width), at),
                pl.BlockSpec((1, rows, width), at),
                pl.BlockSpec((1, rows, width), at),
                pl.BlockSpec((1, heads, rows), plain),
                pl.BlockSpec((1, rows, heads), plain),
                pl.BlockSpec((1, heads, head_dim, head_dim), lambda b, p: (p[b], 0, 0, 0)),
                pl.BlockSpec((heads, head_dim, head_dim), lambda b, p: (0, 0, 0)),
                pl.BlockSpec((1, width), lambda b, p: (0, 0)),
            ],
            out_specs=pl.BlockSpec((1, rows, width), lambda b, p: (p[count + b], 0, 0)),
            scratch_shapes=[pltpu.VMEM((heads, head_dim, head_dim), F32)],
        ),
        out_shape=jax.ShapeDtypeStruct((count, rows, width), BF16),
        name="mix",
    )(pos, q, k, v, cum, cum_t, states, group, gain)


def per_device(tokens, w_query, w_key, w_value, log_decay, norm_gain, w_out, *, n, nh):
    rows, model = tokens.shape
    heads_here = log_decay.shape[0]
    head_dim = w_query.shape[1] // heads_here
    g = math.gcd(heads_here, max(n // 2, 1))
    ng = n // g
    heads = heads_here // g
    width = heads * head_dim
    c = lax.axis_index("ctx")
    h = lax.axis_index("head")
    member = c % g
    group = c // g
    bits = [1 << i for i in range(g.bit_length() - 1)][::-1]
    cube = len(bits) == 3 and ng == 2 and nh == 2
    orders = (bits[:1] + bits[1:][::-1], bits)
    plane = g // 2 if cube else g
    part = (member % plane) * (g // plane) + member // plane

    def exchange(value, where):
        pairs = []
        for a in range(n):
            for b in range(nh):
                to = where(a, b)
                if to is not None:
                    pairs.append((a * nh + b, to[0] * nh + to[1]))
        return lax.ppermute(value, ("ctx", "head"), pairs)

    def spread(value, split, concat, size):
        groups = [[a * size + b for b in range(size)] for a in range(n // size)]
        return lax.all_to_all(
            value, "ctx", split, concat, axis_index_groups=groups, tiled=True
        )

    def over_groups(piece):
        pieces = [piece]
        step = 1
        while step < ng:
            pieces += [exchange(p, lambda a, b: (a ^ (step * g), b)) for p in pieces]
            step *= 2
        return pieces

    def over_planes(piece):
        odd = (c // plane) % 2 == 1
        same = jnp.where(odd, piece[1], piece[0])
        cross = jnp.where(odd, piece[0], piece[1])
        move = lambda x, r: exchange(x, lambda a, b: (a ^ (r * plane), b))
        return [same, move(cross, 1), move(same, 2), move(cross, 3)]

    def true_order(pieces, index):
        if len(pieces) == 1:
            return pieces
        half = len(pieces) // 2
        low, high = true_order(pieces[:half], index), true_order(pieces[half:], index)
        upper = (index & half) != 0
        return [jnp.where(upper, b, a) for a, b in zip(low, high)] + [
            jnp.where(upper, a, b) for a, b in zip(low, high)
        ]

    levels = g // plane
    cumul = jnp.cumsum(log_decay, axis=1).reshape(plane, levels, heads * rows)
    cumul = cumul.transpose(1, 0, 2).reshape(g, heads * rows)
    cumul = spread(cumul, 0, 0, g).reshape(g, heads, rows)
    cum_t = cumul.transpose(0, 2, 1)
    last = cumul[:, :, -1]

    apart = jnp.arange(g, dtype=jnp.int32) ^ member.astype(jnp.int32)

    def place(order):
        out = jnp.zeros_like(apart)
        for i, bit in enumerate(order[::-1]):
            out = out + jnp.where((apart & bit) != 0, 1 << i, 0)
        return out

    def masks(order):
        spots = jnp.arange(g, dtype=jnp.int32)
        out = jnp.zeros_like(spots)
        for i, bit in enumerate(order[::-1]):
            out = out + jnp.where((spots & (1 << i)) != 0, bit, 0)
        return out

    share = model // nh
    own = lax.dynamic_slice_in_dim(tokens, h * share, share, axis=1)[None]
    step_to = lambda stage: (lambda a, b: (a ^ orders[b & 1][stage], b))
    if cube:
        axes = bits
        received = [[bits[0]] + o[1:][::-1] for o in orders]
        odd = (h & 1) == 1
        pos = jnp.where(odd, place(received[1]), place(received[0]))
        block_at = jnp.where(odd, masks(received[1]), masks(received[0])) ^ member
        pos = jnp.concatenate([pos, place(axes)])
        families = []
        for one in (own, exchange(own, step_to(0))):
            two = exchange(one, step_to(1))
            pair = jnp.concatenate([one, two])
            families.append([pair, exchange(pair, step_to(2))])
        families = [f + [exchange(x, lambda a, b: (a, b ^ 1)) for x in f] for f in families]

        def rows_of(weight):
            moved = spread(weight, 1, 0, plane)
            return over_planes([moved[:, :width], moved[:, width:]])

        stack = lambda pieces: jnp.stack(pieces)
        wk, wv, wq = rows_of(w_key), rows_of(w_value), rows_of(w_query)
        turn = jnp.stack([h ^ group, (c // plane) % 2]).astype(jnp.int32)
        wk, wv = stack(wk), stack(wv)
        parts = [
            keys_values(
                jnp.concatenate([block_at[4 * i : 4 * i + 4], turn]), family, wk, wv, cum_t,
                heads, head_dim,
            )
            for i, family in enumerate(families)
        ]
        keys, values, states = (jnp.concatenate(x) for x in zip(*parts))
        early = query_part(turn, *families, stack(wq[:2]), None)
        queries = query_part(turn, *families, stack(wq[2:]), early)
    else:
        axes = orders[0][::-1]
        pos = place(axes)
        block_at = masks(axes) ^ member
        pos = jnp.concatenate([pos, pos])
        for stage in range(len(bits)):
            got = exchange(own, lambda a, b: (a ^ orders[0][stage], b))
            own = jnp.concatenate([own, got], axis=0)
        shares = [own]
        step = 1
        while step < nh:
            shares += [exchange(s, lambda a, b: (a, b ^ step)) for s in shares]
            step *= 2
        full = jnp.concatenate(true_order(shares, h), axis=-1).reshape(g * rows, model)

        def project(weight, act):
            pieces = over_groups(spread(weight, 1, 0, g))
            whole = jnp.concatenate(true_order(pieces, group), axis=0)
            out = act(jnp.dot(full, whole, preferred_element_type=F32)).astype(BF16)
            return out.reshape(g, rows, width)

        keys, values = project(w_key, silu), project(w_value, lambda raw: raw)
        queries = project(w_query, silu)
        states = block_states(block_at, keys, values, cum_t, heads, head_dim)

    through = jnp.cumsum(last, axis=0)
    left = jnp.exp(through[-1] - through)[block_at]
    total = jnp.sum(left[:, :, None, None] * states, axis=0)
    keep = jnp.exp(through[-1])
    later = lambda by: (lambda a, b: (a + by * g, b) if a + by * g < n else None)
    entering = exchange(total, later(1))
    step = 1
    if ng > 2:
        keep = exchange(keep, later(1))
    while step < ng - 1:
        entering = entering + keep[:, None, None] * exchange(entering, later(step))
        keep = keep * exchange(keep, later(step))
        step *= 2

    gain = lax.dynamic_slice_in_dim(norm_gain, part * width, width)[None]
    normed = mix(
        pos, queries, keys, values, cumul, cum_t, states, entering, gain, heads, head_dim
    ).reshape(g * rows, width)
    sides = [normed] + [exchange(normed, lambda a, b: (a, b ^ p)) for p in range(1, nh)]

    out_cols = model // nh
    if cube:
        by_plane = spread(w_out.reshape(plane, levels, width, -1), 0, 0, plane)
        local = by_plane.transpose(1, 2, 0, 3).reshape(levels, width, -1)
        pieces = over_planes(local)
        mine = []
        for p in range(nh):
            side = h ^ p ^ group
            first = jnp.where(side == 0, pieces[0], pieces[2])
            second = jnp.where(side == 0, pieces[1], pieces[3])
            swap = (c // plane) % 2 == 1
            mine.append(
                jnp.concatenate(
                    [jnp.where(swap, second, first), jnp.where(swap, first, second)], axis=1
                )
            )
    else:
        local = spread(w_out.reshape(g, width, -1), 0, 0, g)
        local = local.transpose(1, 0, 2).reshape(width, -1)
        whole = jnp.concatenate(true_order(over_groups(local), group), axis=1)
        whole = whole.reshape(width, nh, out_cols).transpose(1, 0, 2)
        mine = [lax.dynamic_index_in_dim(whole, h ^ p, 0, False) for p in range(nh)]
    right = mine[:1] + [exchange(m, lambda a, b: (a, b ^ (p + 1))) for p, m in enumerate(mine[1:])]
    partial = sum(
        jnp.dot(t, w, preferred_element_type=F32) for t, w in zip(sides, right)
    ).astype(BF16)

    chunks = max(len(bits), 1)
    span = out_cols // chunks
    summed = []
    for j in range(chunks):
        piece = partial[:, j * span : (j + 1) * span].reshape((2,) * len(bits) + (rows, -1))
        left_bits = list(axes)
        for bit in bits[j:] + bits[:j]:
            axis = left_bits.index(bit)
            left_bits.pop(axis)
            kept = lax.index_in_dim(piece, 0, axis, False)
            sent = lax.index_in_dim(piece, 1, axis, False)
            got = exchange(sent, lambda a, b: (a ^ bit, b))
            piece = (kept.astype(F32) + got.astype(F32)).astype(BF16)
        summed.append(piece)
    return jnp.concatenate(summed, axis=1)


def solution(mesh):
    placed = (
        P("ctx", None),
        P("ctx", "head"),
        P("ctx", "head"),
        P("ctx", "head"),
        P("head", "ctx"),
        P("head"),
        P("head", "ctx"),
    )
    body = functools.partial(per_device, n=mesh.shape["ctx"], nh=mesh.shape["head"])

    return jax.shard_map(
        body, mesh=mesh, in_specs=placed, out_specs=P("ctx", "head"), check_vma=False
    )
```

```python
import functools
import math

import jax
import jax.numpy as jnp
from jax import lax
from jax.experimental import pallas as pl
from jax.experimental.pallas import tpu as pltpu
from jax.sharding import PartitionSpec as P


F32 = jnp.float32
BF16 = jnp.bfloat16


def silu(x):
    return x / (1.0 + jnp.exp(-x))


def block_state(k, v, cum_t, heads, head_dim):
    rows = k.shape[0]
    out = []
    for i in range(heads):
        cols = slice(i * head_dim, (i + 1) * head_dim)
        cum = cum_t[:, i : i + 1]
        last = cum_t[rows - 1 : rows, i : i + 1]
        decayed = (k[:, cols].astype(F32) * jnp.exp(last - cum)).astype(BF16)
        out.append(
            lax.dot_general(
                decayed, v[:, cols], (((0,), (0,)), ((), ())), preferred_element_type=F32
            )
        )
    return out


def state_body(where, k_ref, v_ref, cum_t_ref, out_ref, *, heads, head_dim):
    for i, s in enumerate(block_state(k_ref[0], v_ref[0], cum_t_ref[0], heads, head_dim)):
        out_ref[0, i] = s


def block_states(block_at, k, v, cum_t, heads, head_dim):
    count, rows, width = k.shape
    here = lambda i, w: (i, 0, 0)
    return pl.pallas_call(
        functools.partial(state_body, heads=heads, head_dim=head_dim),
        grid_spec=pltpu.PrefetchScalarGridSpec(
            num_scalar_prefetch=1,
            grid=(count,),
            in_specs=[
                pl.BlockSpec((1, rows, width), here),
                pl.BlockSpec((1, rows, width), here),
                pl.BlockSpec((1, rows, heads), lambda i, w: (w[i], 0, 0)),
            ],
            out_specs=pl.BlockSpec(
                (1, heads, head_dim, head_dim), lambda i, w: (i, 0, 0, 0)
            ),
        ),
        out_shape=jax.ShapeDtypeStruct((count, heads, head_dim, head_dim), F32),
        name="block_states",
    )(block_at, k, v, cum_t)


OWN = ((0, 0, 0), (0, 1, 1), (1, 0, 2), (1, 1, 3))
OTHER = ((0, 0, 0), (0, 1, 2), (1, 0, 1), (1, 1, 3))


def wide(ref):
    return ref[...].reshape(-1, ref.shape[-1])


def stand_up(cum_ref, cum_t_ref):
    count, _, heads = cum_t_ref.shape
    turned = cum_ref[...].T
    for i in range(count):
        cum_t_ref[i] = turned[:, i * heads : (i + 1) * heads]


def keys_values_body(table, *refs, heads, head_dim):
    tokens, weights = refs[:8], refs[8:16]
    cum_ref, after_ref, k_ref, v_ref, state_ref, total_ref, w_ref, cum_t_ref = refs[16:]
    stand_up(cum_ref, cum_t_ref)
    rows, width = k_ref.shape[1:]
    cut = weights[0].shape[0]
    mine, swap = table[8], table[9]
    for side in range(2):
        for i in range(2):
            for r in range(4):

                @pl.when(2 * (mine ^ side) + (swap ^ i) == r)
                def _():
                    for j in range(2):
                        w_ref[side, i * cut : (i + 1) * cut, j * width : (j + 1) * width] = (
                            weights[4 * j + r][...]
                        )

    totals = [0.0] * heads
    for family in range(2):
        out = [
            jnp.dot(wide(x), w_ref[i // 2], preferred_element_type=F32)
            for i, x in enumerate(tokens[4 * family : 4 * family + 4])
        ]
        block = lambda x, at: x[at[0]][at[1] * rows : (at[1] + 1) * rows]
        for spot in range(4):
            mate = [at for at in OTHER if at[2] == spot][0]
            raw = block(out[:2], OWN[spot]) + block(out[2:], mate)
            k = silu(raw[:, :width]).astype(BF16)
            v = raw[:, width:].astype(BF16)
            at = 4 * family + spot
            k_ref[at] = k
            v_ref[at] = v
            b = table[at]
            for i, s in enumerate(block_state(k, v, cum_t_ref[b], heads, head_dim)):
                state_ref[at, i] = s
                totals[i] += jnp.exp(after_ref[b, :, i : i + 1]) * s
    for i in range(heads):
        total_ref[i] = totals[i]


def on_chip(count):
    return [pl.BlockSpec(memory_space=pltpu.VMEM) for _ in range(count)]


def keys_values(table, near, far, wk, wv, cum, after, heads, head_dim):
    _, rows, _ = near[0].shape
    cut, width = wk[0].shape
    return pl.pallas_call(
        functools.partial(keys_values_body, heads=heads, head_dim=head_dim),
        in_specs=[pl.BlockSpec(memory_space=pltpu.SMEM)] + on_chip(18),
        out_specs=on_chip(4),
        out_shape=[
            jax.ShapeDtypeStruct((8, rows, width), BF16),
            jax.ShapeDtypeStruct((8, rows, width), BF16),
            jax.ShapeDtypeStruct((8, heads, head_dim, head_dim), F32),
            jax.ShapeDtypeStruct((heads, head_dim, head_dim), F32),
        ],
        scratch_shapes=[
            pltpu.VMEM((2, 2 * cut, 2 * width), BF16),
            pltpu.VMEM((8, rows, heads), F32),
        ],
        name="keys_values",
    )(table, *near, *far, *wk, *wv, cum, after)


def query_body(table, *refs, late):
    tokens, (first, second, *rest, out_ref, w_ref) = refs[:8], refs[8:]
    rows = out_ref.shape[1]
    cut = first.shape[0]
    mine, swap = table[0], table[1]
    for i, (low, high) in enumerate(((first, second), (second, first))):

        @pl.when(swap == i)
        def _():
            w_ref[:cut] = low[...]
            w_ref[cut:] = high[...]

    for side, spots in ((0, OWN), (1, OTHER)):

        @pl.when((mine ^ side) == (1 if late else 0))
        def _():
            for family in range(2):
                runs = tokens[4 * family + 2 * side : 4 * family + 2 * side + 2]
                out = [jnp.dot(wide(x), w_ref[...], preferred_element_type=F32) for x in runs]
                for run, index, spot in spots:
                    part = out[run][index * rows : (index + 1) * rows]
                    at = 4 * family + spot
                    if late:
                        out_ref[at] = silu(rest[0][at] + part).astype(BF16)
                    else:
                        out_ref[at] = part


def query_part(table, near, far, weights, early):
    _, rows, _ = near[0].shape
    cut, width = weights[0].shape
    late = early is not None
    args = [*near, *far, *weights] + ([early] if late else [])
    return pl.pallas_call(
        functools.partial(query_body, late=late),
        in_specs=[pl.BlockSpec(memory_space=pltpu.SMEM)] + on_chip(len(args)),
        out_specs=on_chip(1)[0],
        out_shape=jax.ShapeDtypeStruct((8, rows, width), BF16 if late else F32),
        scratch_shapes=[pltpu.VMEM((2 * cut, width), BF16)],
    )(table, *args)


def mix_body(
    table, q_ref, k_ref, v_ref, cum_ref, state_ref, group_ref, gain_ref, out_ref, cum_t_ref,
    *, heads, head_dim,
):
    count, rows = q_ref.shape[:2]
    causal = lax.broadcasted_iota(jnp.int32, (rows, rows), 0) >= lax.broadcasted_iota(
        jnp.int32, (rows, rows), 1
    )
    stand_up(cum_ref, cum_t_ref)
    carry = [group_ref[i] for i in range(heads)]
    for b in range(count):
        at, to, order = table[b], table[count + b], table[2 * count + b]
        for i in range(heads):
            cols = slice(i * head_dim, (i + 1) * head_dim)
            q, k, v = q_ref[at, :, cols], k_ref[at, :, cols], v_ref[at, :, cols]
            cum = cum_t_ref[order, :, i : i + 1]
            last = cum_t_ref[order, rows - 1 : rows, i : i + 1]
            diff = cum - cum_ref[pl.ds(order * heads + i, 1), :]
            decay = jnp.where(causal, jnp.exp(jnp.where(causal, diff, 0.0)), 0.0)
            scores = lax.dot_general(q, k, (((1,), (1,)), ((), ())), preferred_element_type=F32)
            weights = (scores * decay).astype(BF16)
            intra = jnp.dot(weights, v, preferred_element_type=F32)
            state = carry[i]
            carry[i] = jnp.exp(last) * state + state_ref[at, i]
            high = state.astype(BF16)
            low = (state - high.astype(F32)).astype(BF16)
            inter = jnp.dot(q, high, preferred_element_type=F32) + jnp.dot(
                q, low, preferred_element_type=F32
            )
            mixed = intra + jnp.exp(cum) * inter
            scale = lax.rsqrt(jnp.mean(mixed * mixed, axis=-1, keepdims=True) + 1e-06)
            out_ref[to, :, cols] = (mixed * scale * gain_ref[:, cols]).astype(BF16)


def mix(table, q, k, v, cum, states, group, gain, heads, head_dim):
    return pl.pallas_call(
        functools.partial(mix_body, heads=heads, head_dim=head_dim),
        in_specs=[pl.BlockSpec(memory_space=pltpu.SMEM)] + on_chip(7),
        out_specs=on_chip(1)[0],
        out_shape=jax.ShapeDtypeStruct(k.shape, BF16),
        scratch_shapes=[pltpu.VMEM((k.shape[0], k.shape[1], heads), F32)],
        name="mix",
    )(table, q, k, v, cum, states, group, gain)


def per_device(tokens, w_query, w_key, w_value, log_decay, norm_gain, w_out, *, n, nh):
    rows, model = tokens.shape
    heads_here = log_decay.shape[0]
    head_dim = w_query.shape[1] // heads_here
    g = math.gcd(heads_here, max(n // 2, 1))
    ng = n // g
    heads = heads_here // g
    width = heads * head_dim
    c = lax.axis_index("ctx")
    h = lax.axis_index("head")
    member = c % g
    group = c // g
    bits = [1 << i for i in range(g.bit_length() - 1)][::-1]
    cube = len(bits) == 3 and ng == 2 and nh == 2
    orders = (bits[:1] + bits[1:][::-1], bits)
    plane = g // 2 if cube else g
    part = (member % plane) * (g // plane) + member // plane

    def exchange(value, where):
        pairs = []
        for a in range(n):
            for b in range(nh):
                to = where(a, b)
                if to is not None:
                    pairs.append((a * nh + b, to[0] * nh + to[1]))
        return lax.ppermute(value, ("ctx", "head"), pairs)

    def spread(value, split, concat, size):
        groups = [[a * size + b for b in range(size)] for a in range(n // size)]
        return lax.all_to_all(
            value, "ctx", split, concat, axis_index_groups=groups, tiled=True
        )

    def over_groups(piece):
        pieces = [piece]
        step = 1
        while step < ng:
            pieces += [exchange(p, lambda a, b: (a ^ (step * g), b)) for p in pieces]
            step *= 2
        return pieces

    def over_planes(piece):
        odd = (c // plane) % 2 == 1
        same = jnp.where(odd, piece[1], piece[0])
        cross = jnp.where(odd, piece[0], piece[1])
        move = lambda x, r: exchange(x, lambda a, b: (a ^ (r * plane), b))
        return [same, move(cross, 1), move(same, 2), move(cross, 3)]

    def true_order(pieces, index):
        if len(pieces) == 1:
            return pieces
        half = len(pieces) // 2
        low, high = true_order(pieces[:half], index), true_order(pieces[half:], index)
        upper = (index & half) != 0
        return [jnp.where(upper, b, a) for a, b in zip(low, high)] + [
            jnp.where(upper, a, b) for a, b in zip(low, high)
        ]

    levels = g // plane
    spots = jnp.arange(rows)
    upto = (spots[:, None] <= spots[None, :]).astype(F32)
    cumul = jnp.dot(
        log_decay, upto, precision=lax.Precision.HIGHEST, preferred_element_type=F32
    ).reshape(plane, levels, heads * rows)
    if cube:
        odd = (c // plane) % 2 == 1
        keep = jnp.where(odd, cumul[:, 1], cumul[:, 0])
        give = jnp.where(odd, cumul[:, 0], cumul[:, 1])
        got = exchange(give, lambda a, b: (a ^ plane, b))
        both = jnp.concatenate(
            [keep.reshape(plane, heads, rows), got.reshape(plane, heads, rows)], axis=1
        ).reshape(g * heads, rows)
        cumul = spread(both, 0, 0, plane)
    else:
        cumul = cumul.transpose(1, 0, 2).reshape(g * heads, rows)
        cumul = spread(cumul, 0, 0, g)
    last = cumul[:, -1].reshape(g, heads)

    def entry(a, b):
        received = [bits[0]] + orders[b & 1][1:][::-1] if cube else orders[0][::-1]
        regular = bits if cube else received
        mask = lambda order, spot: sum(
            bit for i, bit in enumerate(order[::-1]) if spot >> i & 1
        )
        at = [mask(received, spot) ^ (a % g) for spot in range(g)]
        to = [mask(regular, spot) ^ (a % g) for spot in range(g)]
        where = [at.index(k) for k in range(g)] + [to.index(k) for k in range(g)]
        shift = (a // plane) % 2 if cube else 0
        decays = [(k % plane) * levels + (k // plane ^ shift) for k in range(g)]
        side = [b ^ (a // g), (a // plane) % 2]
        return [decays[k] for k in at] + where + decays + [decays.index(k) for k in range(g)] + side

    entries = jnp.array([entry(a, b) for a in range(n) for b in range(nh)], jnp.int32)
    table = lax.dynamic_index_in_dim(entries, c * nh + h, 0, False)
    decays_at, pos, turn = table[:g], table[g : 4 * g], table[5 * g :]
    ends = table[4 * g : 5 * g]
    after = jnp.sum(
        jnp.where((ends[:, None] < ends[None, :])[:, :, None], last[None], 0.0), axis=1
    )[:, None, :]
    tables = [jnp.concatenate([decays_at, turn]), turn, pos]
    gain = lax.dynamic_slice_in_dim(norm_gain, part * width, width)[None]

    share = model // nh
    own = lax.dynamic_slice_in_dim(tokens, h * share, share, axis=1)[None]
    step_to = lambda stage: (lambda a, b: (a ^ orders[b & 1][stage], b))
    if cube:
        axes = bits
        families = []
        for name, one in (("near", own), ("far", exchange(own, step_to(0)))):
            two = exchange(one, step_to(1))
            if name == "far":
                two, tables, gain = lax.optimization_barrier((two, tables, gain))
            pair = jnp.concatenate([one, two])
            families.append([pair, exchange(pair, step_to(2))])
        families = [f + [exchange(x, lambda a, b: (a, b ^ 1)) for x in f] for f in families]

        def rows_of(weight):
            moved = spread(weight, 1, 0, plane)
            return over_planes([moved[:, :width], moved[:, width:]])

        wk, wv, wq = rows_of(w_key), rows_of(w_value), rows_of(w_query)
        keys, values, states, total = keys_values(
            tables[0], *families, wk, wv, cumul, after, heads, head_dim
        )
        early = query_part(tables[1], *families, wq[:2], None)
        queries = query_part(tables[1], *families, wq[2:], early)
    else:
        axes = orders[0][::-1]
        for stage in range(len(bits)):
            got = exchange(own, lambda a, b: (a ^ orders[0][stage], b))
            own = jnp.concatenate([own, got], axis=0)
        shares = [own]
        step = 1
        while step < nh:
            shares += [exchange(s, lambda a, b: (a, b ^ step)) for s in shares]
            step *= 2
        full = jnp.concatenate(true_order(shares, h), axis=-1).reshape(g * rows, model)

        def project(weight, act):
            pieces = over_groups(spread(weight, 1, 0, g))
            whole = jnp.concatenate(true_order(pieces, group), axis=0)
            out = act(jnp.dot(full, whole, preferred_element_type=F32)).astype(BF16)
            return out.reshape(g, rows, width)

        keys, values = project(w_key, silu), project(w_value, lambda raw: raw)
        queries = project(w_query, silu)
        cum_t = cumul.reshape(g, heads, rows).transpose(0, 2, 1)
        states = block_states(decays_at, keys, values, cum_t, heads, head_dim)
        total = jnp.sum(jnp.exp(after[:, 0])[decays_at][:, :, None, None] * states, axis=0)

    keep = jnp.exp(jnp.sum(last, axis=0))
    later = lambda by: (lambda a, b: (a + by * g, b) if a + by * g < n else None)
    entering = exchange(total, later(1))
    step = 1
    if ng > 2:
        keep = exchange(keep, later(1))
    while step < ng - 1:
        entering = entering + keep[:, None, None] * exchange(entering, later(step))
        keep = keep * exchange(keep, later(step))
        step *= 2

    normed = mix(
        tables[2], queries, keys, values, cumul, states, entering, gain, heads, head_dim
    ).reshape(g * rows, width)
    sides = [normed] + [exchange(normed, lambda a, b: (a, b ^ p)) for p in range(1, nh)]

    out_cols = model // nh
    parts = 2 if cube else 1
    if cube:
        by_plane = spread(w_out, 0, 0, plane)
        by_plane = lax.optimization_barrier((by_plane, total))[0]
        by_plane = by_plane.reshape(plane, levels, width, -1)
        local = by_plane.transpose(1, 2, 0, 3).reshape(levels, width, -1)
        cut = local.shape[-1] // parts
        cuts = lax.optimization_barrier(
            [local[:, :, i * cut : (i + 1) * cut] for i in range(parts)]
        )
        swap = (c // plane) % 2 == 1
        mine = []
        for x in cuts:
            pieces = over_planes(x)
            mine.append([])
            for p in range(nh):
                side = h ^ p ^ group
                first = jnp.where(side == 0, pieces[0], pieces[2])
                second = jnp.where(side == 0, pieces[1], pieces[3])
                ordered = [jnp.where(swap, second, first), jnp.where(swap, first, second)]
                mine[-1].append(jnp.concatenate(ordered, axis=1))
    else:
        local = spread(w_out.reshape(g, width, -1), 0, 0, g)
        local = local.transpose(1, 0, 2).reshape(width, -1)
        whole = jnp.concatenate(true_order(over_groups(local), group), axis=1)
        whole = whole.reshape(width, nh, out_cols).transpose(1, 0, 2)
        mine = [[lax.dynamic_index_in_dim(whole, h ^ p, 0, False) for p in range(nh)]]

    done = []
    for columns in mine:
        right = columns[:1] + [
            exchange(m, lambda a, b: (a, b ^ (p + 1)))
            for p, m in enumerate(columns[1:])
        ]
        partial = sum(
            jnp.dot(t, w, preferred_element_type=F32) for t, w in zip(sides, right)
        ).astype(BF16)
        chunks = max(len(bits), 1)
        span = partial.shape[1] // chunks
        summed = []
        for j in range(chunks):
            piece = partial[:, j * span : (j + 1) * span].reshape((2,) * len(bits) + (rows, -1))
            left = list(axes)
            for stage, bit in enumerate(bits[j:] + bits[:j]):
                axis = left.index(bit)
                left.pop(axis)
                kept = lax.index_in_dim(piece, 0, axis, False)
                sent = lax.index_in_dim(piece, 1, axis, False)
                got = exchange(sent, lambda a, b: (a ^ bit, b))
                piece = (kept.astype(F32) + got.astype(F32)).astype(BF16)
            summed.append(piece)
        done.append(jnp.concatenate(summed, axis=1))
    if cube:
        done = [d[:, i * cut : (i + 1) * cut] for i in range(2) for d in done]
    return jnp.concatenate(done, axis=1)


def solution(mesh):
    placed = (
        P("ctx", None),
        P("ctx", "head"),
        P("ctx", "head"),
        P("ctx", "head"),
        P("head", "ctx"),
        P("head"),
        P("head", "ctx"),
    )
    body = functools.partial(per_device, n=mesh.shape["ctx"], nh=mesh.shape["head"])

    return jax.shard_map(
        body, mesh=mesh, in_specs=placed, out_specs=P("ctx", "head"), check_vma=False
    )
```

```python
import functools
import math

import jax
import jax.numpy as jnp
from jax import lax
from jax.experimental import pallas as pl
from jax.experimental.pallas import tpu as pltpu
from jax.sharding import PartitionSpec as P


F32 = jnp.float32
BF16 = jnp.bfloat16


def silu(x):
    return x / (1.0 + jnp.exp(-x))


def block_state(k, v, cum_t, heads, head_dim):
    rows = k.shape[0]
    out = []
    for i in range(heads):
        cols = slice(i * head_dim, (i + 1) * head_dim)
        cum = cum_t[:, i : i + 1]
        last = cum_t[rows - 1 : rows, i : i + 1]
        decayed = (k[:, cols].astype(F32) * jnp.exp(last - cum)).astype(BF16)
        out.append(
            lax.dot_general(
                decayed, v[:, cols], (((0,), (0,)), ((), ())), preferred_element_type=F32
            )
        )
    return out


def state_body(where, k_ref, v_ref, cum_t_ref, out_ref, *, heads, head_dim):
    for i, s in enumerate(block_state(k_ref[0], v_ref[0], cum_t_ref[0], heads, head_dim)):
        out_ref[0, i] = s


def block_states(block_at, k, v, cum_t, heads, head_dim):
    count, rows, width = k.shape
    here = lambda i, w: (i, 0, 0)
    return pl.pallas_call(
        functools.partial(state_body, heads=heads, head_dim=head_dim),
        grid_spec=pltpu.PrefetchScalarGridSpec(
            num_scalar_prefetch=1,
            grid=(count,),
            in_specs=[
                pl.BlockSpec((1, rows, width), here),
                pl.BlockSpec((1, rows, width), here),
                pl.BlockSpec((1, rows, heads), lambda i, w: (w[i], 0, 0)),
            ],
            out_specs=pl.BlockSpec(
                (1, heads, head_dim, head_dim), lambda i, w: (i, 0, 0, 0)
            ),
        ),
        out_shape=jax.ShapeDtypeStruct((count, heads, head_dim, head_dim), F32),
        name="block_states",
    )(block_at, k, v, cum_t)


OWN = ((0, 0, 0), (0, 1, 1), (1, 0, 2), (1, 1, 3))
OTHER = ((0, 0, 0), (0, 1, 2), (1, 0, 1), (1, 1, 3))


def wide(ref):
    return ref[...].reshape(-1, ref.shape[-1])


def stand_up(cum_ref, cum_t_ref):
    count, _, heads = cum_t_ref.shape
    turned = cum_ref[...].T
    for i in range(count):
        cum_t_ref[i] = turned[:, i * heads : (i + 1) * heads]


def keys_values_body(table, *refs, heads, head_dim):
    tokens, weights, (first, second) = refs[:8], refs[8:16], refs[16:18]
    cum_ref, k_ref, v_ref, state_ref, total_ref, early_ref, w_ref, cum_t_ref = refs[18:]
    stand_up(cum_ref, cum_t_ref)
    count, rows, width = k_ref.shape
    cut = weights[0].shape[0]
    mine, swap = table[8], table[9]
    for side in range(2):
        for i in range(2):
            span = slice(i * cut, (i + 1) * cut)
            for r in range(4):

                @pl.when(2 * (mine ^ side) + (swap ^ i) == r)
                def _():
                    for j in range(2):
                        w_ref[side, span, j * width : (j + 1) * width] = weights[4 * j + r][...]
                    w_ref[side, span, 2 * width :] = (
                        (first, second)[r][...] if r < 2 else jnp.zeros((cut, width), BF16)
                    )

    for family in range(2):
        out = [
            jnp.dot(wide(x), w_ref[i // 2], preferred_element_type=F32)
            for i, x in enumerate(tokens[4 * family : 4 * family + 4])
        ]
        block = lambda x, at: x[at[0]][at[1] * rows : (at[1] + 1) * rows]
        for spot in range(4):
            mate = [at for at in OTHER if at[2] == spot][0]
            raw = block(out[:2], OWN[spot]) + block(out[2:], mate)
            k = silu(raw[:, :width]).astype(BF16)
            v = raw[:, width : 2 * width].astype(BF16)
            at = 4 * family + spot
            k_ref[at] = k
            v_ref[at] = v
            early_ref[at] = raw[:, 2 * width :]
            b = table[at]
            for i, s in enumerate(block_state(k, v, cum_t_ref[b], heads, head_dim)):
                state_ref[at, i] = s
    for i in range(heads):
        total = jnp.zeros(total_ref.shape[1:], F32)
        for b in range(count):
            at, order = table[10 + b], table[10 + 2 * count + b]
            last = cum_t_ref[order, rows - 1 : rows, i : i + 1]
            total = jnp.exp(last) * total + state_ref[at, i]
        total_ref[i] = total


def on_chip(count):
    return [pl.BlockSpec(memory_space=pltpu.VMEM) for _ in range(count)]


def keys_values(table, near, far, wk, wv, wq, cum, heads, head_dim):
    _, rows, _ = near[0].shape
    cut, width = wk[0].shape
    return pl.pallas_call(
        functools.partial(keys_values_body, heads=heads, head_dim=head_dim),
        in_specs=[pl.BlockSpec(memory_space=pltpu.SMEM)] + on_chip(19),
        out_specs=on_chip(5),
        out_shape=[
            jax.ShapeDtypeStruct((8, rows, width), BF16),
            jax.ShapeDtypeStruct((8, rows, width), BF16),
            jax.ShapeDtypeStruct((8, heads, head_dim, head_dim), F32),
            jax.ShapeDtypeStruct((heads, head_dim, head_dim), F32),
            jax.ShapeDtypeStruct((8, rows, width), F32),
        ],
        scratch_shapes=[
            pltpu.VMEM((2, 2 * cut, 3 * width), BF16),
            pltpu.VMEM((8, rows, heads), F32),
        ],
        name="keys_values",
    )(table, *near, *far, *wk, *wv, *wq, cum)


def query_body(table, *refs):
    tokens, (first, second, early_ref, out_ref, w_ref) = refs[:8], refs[8:]
    rows = out_ref.shape[1]
    cut = first.shape[0]
    mine, swap = table[0], table[1]
    for i, (low, high) in enumerate(((first, second), (second, first))):

        @pl.when(swap == i)
        def _():
            w_ref[:cut] = low[...]
            w_ref[cut:] = high[...]

    for side, spots in ((0, OWN), (1, OTHER)):

        @pl.when((mine ^ side) == 1)
        def _():
            for family in range(2):
                runs = tokens[4 * family + 2 * side : 4 * family + 2 * side + 2]
                out = [jnp.dot(wide(x), w_ref[...], preferred_element_type=F32) for x in runs]
                for run, index, spot in spots:
                    part = out[run][index * rows : (index + 1) * rows]
                    at = 4 * family + spot
                    out_ref[at] = silu(early_ref[at] + part).astype(BF16)


def late_queries(table, near, far, weights, early):
    _, rows, _ = near[0].shape
    cut, width = weights[0].shape
    return pl.pallas_call(
        query_body,
        in_specs=[pl.BlockSpec(memory_space=pltpu.SMEM)] + on_chip(11),
        out_specs=on_chip(1)[0],
        out_shape=jax.ShapeDtypeStruct((8, rows, width), BF16),
        scratch_shapes=[pltpu.VMEM((2 * cut, width), BF16)],
        name="late_q",
    )(table, *near, *far, *weights, early)


def mix_body(
    table, q_ref, k_ref, v_ref, cum_ref, state_ref, group_ref, gain_ref, out_ref, cum_t_ref,
    *, heads, head_dim,
):
    count, rows = q_ref.shape[:2]
    causal = lax.broadcasted_iota(jnp.int32, (rows, rows), 0) >= lax.broadcasted_iota(
        jnp.int32, (rows, rows), 1
    )
    stand_up(cum_ref, cum_t_ref)
    carry = [jnp.where(table[3 * count] > 0, group_ref[i], 0.0) for i in range(heads)]
    for b in range(count):
        at, to, order = table[b], table[count + b], table[2 * count + b]
        for i in range(heads):
            cols = slice(i * head_dim, (i + 1) * head_dim)
            q, k, v = q_ref[at, :, cols], k_ref[at, :, cols], v_ref[at, :, cols]
            cum = cum_t_ref[order, :, i : i + 1]
            last = cum_t_ref[order, rows - 1 : rows, i : i + 1]
            diff = cum - cum_ref[pl.ds(order * heads + i, 1), :]
            decay = jnp.where(causal, jnp.exp(jnp.where(causal, diff, 0.0)), 0.0)
            scores = lax.dot_general(q, k, (((1,), (1,)), ((), ())), preferred_element_type=F32)
            weights = (scores * decay).astype(BF16)
            intra = jnp.dot(weights, v, preferred_element_type=F32)
            state = carry[i]
            carry[i] = jnp.exp(last) * state + state_ref[at, i]
            high = state.astype(BF16)
            low = (state - high.astype(F32)).astype(BF16)
            inter = jnp.dot(q, high, preferred_element_type=F32) + jnp.dot(
                q, low, preferred_element_type=F32
            )
            mixed = intra + jnp.exp(cum) * inter
            scale = lax.rsqrt(jnp.mean(mixed * mixed, axis=-1, keepdims=True) + 1e-06)
            out_ref[to, :, cols] = (mixed * scale * gain_ref[:, cols]).astype(BF16)


def mix(table, q, k, v, cum, states, group, gain, heads, head_dim):
    return pl.pallas_call(
        functools.partial(mix_body, heads=heads, head_dim=head_dim),
        in_specs=[pl.BlockSpec(memory_space=pltpu.SMEM)] + on_chip(7),
        out_specs=on_chip(1)[0],
        out_shape=jax.ShapeDtypeStruct(k.shape, BF16),
        scratch_shapes=[pltpu.VMEM((k.shape[0], k.shape[1], heads), F32)],
        name="mix",
    )(table, q, k, v, cum, states, group, gain)


def per_device(tokens, w_query, w_key, w_value, log_decay, norm_gain, w_out, *, n, nh):
    rows, model = tokens.shape
    heads_here = log_decay.shape[0]
    head_dim = w_query.shape[1] // heads_here
    g = math.gcd(heads_here, max(n // 2, 1))
    ng = n // g
    heads = heads_here // g
    width = heads * head_dim
    c = lax.axis_index("ctx")
    h = lax.axis_index("head")
    member = c % g
    group = c // g
    bits = [1 << i for i in range(g.bit_length() - 1)][::-1]
    cube = len(bits) == 3 and ng == 2 and nh == 2
    orders = (bits[:1] + bits[1:][::-1], bits)
    plane = g // 2 if cube else g
    part = (member % plane) * (g // plane) + member // plane

    def exchange(value, where):
        pairs = []
        for a in range(n):
            for b in range(nh):
                to = where(a, b)
                if to is not None:
                    pairs.append((a * nh + b, to[0] * nh + to[1]))
        return lax.ppermute(value, ("ctx", "head"), pairs)

    def spread(value, split, concat, size):
        groups = [[a * size + b for b in range(size)] for a in range(n // size)]
        return lax.all_to_all(
            value, "ctx", split, concat, axis_index_groups=groups, tiled=True
        )

    def over_groups(piece):
        pieces = [piece]
        step = 1
        while step < ng:
            pieces += [exchange(p, lambda a, b: (a ^ (step * g), b)) for p in pieces]
            step *= 2
        return pieces

    def over_planes(piece):
        odd = (c // plane) % 2 == 1
        same = jnp.where(odd, piece[1], piece[0])
        cross = jnp.where(odd, piece[0], piece[1])
        move = lambda x, r: exchange(x, lambda a, b: (a ^ (r * plane), b))
        return [same, move(cross, 1), move(same, 2), move(cross, 3)]

    def true_order(pieces, index):
        if len(pieces) == 1:
            return pieces
        half = len(pieces) // 2
        low, high = true_order(pieces[:half], index), true_order(pieces[half:], index)
        upper = (index & half) != 0
        return [jnp.where(upper, b, a) for a, b in zip(low, high)] + [
            jnp.where(upper, a, b) for a, b in zip(low, high)
        ]

    levels = g // plane
    spots = jnp.arange(rows)
    upto = (spots[:, None] <= spots[None, :]).astype(F32)
    cumul = jnp.dot(
        log_decay, upto, precision=lax.Precision.HIGHEST, preferred_element_type=F32
    ).reshape(plane, levels, heads * rows)
    if cube:
        odd = (c // plane) % 2 == 1
        keep = jnp.where(odd, cumul[:, 1], cumul[:, 0])
        give = jnp.where(odd, cumul[:, 0], cumul[:, 1])
        got = exchange(give, lambda a, b: (a ^ plane, b))
        both = jnp.concatenate(
            [keep.reshape(plane, heads, rows), got.reshape(plane, heads, rows)], axis=1
        ).reshape(g * heads, rows)
        cumul = spread(both, 0, 0, plane)
    else:
        cumul = cumul.transpose(1, 0, 2).reshape(g * heads, rows)
        cumul = spread(cumul, 0, 0, g)
    last = cumul[:, -1].reshape(g, heads)

    def entry(a, b):
        received = [bits[0]] + orders[b & 1][1:][::-1] if cube else orders[0][::-1]
        regular = bits if cube else received
        mask = lambda order, spot: sum(
            bit for i, bit in enumerate(order[::-1]) if spot >> i & 1
        )
        at = [mask(received, spot) ^ (a % g) for spot in range(g)]
        to = [mask(regular, spot) ^ (a % g) for spot in range(g)]
        where = [at.index(k) for k in range(g)] + [to.index(k) for k in range(g)]
        shift = (a // plane) % 2 if cube else 0
        decays = [(k % plane) * levels + (k // plane ^ shift) for k in range(g)]
        side = [b ^ (a // g), (a // plane) % 2]
        return [decays[k] for k in at] + where + decays + [decays.index(k) for k in range(g)] + side

    entries = jnp.array([entry(a, b) for a in range(n) for b in range(nh)], jnp.int32)
    table = lax.dynamic_index_in_dim(entries, c * nh + h, 0, False)
    decays_at, pos, turn = table[:g], table[g : 4 * g], table[5 * g :]
    tables = [jnp.concatenate([decays_at, turn, pos]), turn]
    tables.append(jnp.concatenate([pos, jnp.stack([group]).astype(jnp.int32)]))
    gain = lax.dynamic_slice_in_dim(norm_gain, part * width, width)[None]

    share = model // nh
    own = lax.dynamic_slice_in_dim(tokens, h * share, share, axis=1)[None]
    step_to = lambda stage: (lambda a, b: (a ^ orders[b & 1][stage], b))
    if cube:
        axes = bits
        families = []
        for name, one in (("near", own), ("far", exchange(own, step_to(0)))):
            two = exchange(one, step_to(1))
            if name == "far":
                two, tables, gain = lax.optimization_barrier((two, tables, gain))
            pair = jnp.concatenate([one, two])
            families.append([pair, exchange(pair, step_to(2))])
        families = [f + [exchange(x, lambda a, b: (a, b ^ 1)) for x in f] for f in families]

        def rows_of(weight):
            moved = spread(weight, 1, 0, plane)
            return over_planes([moved[:, :width], moved[:, width:]])

        wk, wv, wq = rows_of(w_key), rows_of(w_value), rows_of(w_query)
        keys, values, states, total, early = keys_values(
            tables[0], *families, wk, wv, wq[:2], cumul, heads, head_dim
        )
        queries = late_queries(tables[1], *families, wq[2:], early)
    else:
        axes = orders[0][::-1]
        for stage in range(len(bits)):
            got = exchange(own, lambda a, b: (a ^ orders[0][stage], b))
            own = jnp.concatenate([own, got], axis=0)
        shares = [own]
        step = 1
        while step < nh:
            shares += [exchange(s, lambda a, b: (a, b ^ step)) for s in shares]
            step *= 2
        full = jnp.concatenate(true_order(shares, h), axis=-1).reshape(g * rows, model)

        def project(weight, act):
            pieces = over_groups(spread(weight, 1, 0, g))
            whole = jnp.concatenate(true_order(pieces, group), axis=0)
            out = act(jnp.dot(full, whole, preferred_element_type=F32)).astype(BF16)
            return out.reshape(g, rows, width)

        keys, values = project(w_key, silu), project(w_value, lambda raw: raw)
        queries = project(w_query, silu)
        cum_t = cumul.reshape(g, heads, rows).transpose(0, 2, 1)
        states = block_states(decays_at, keys, values, cum_t, heads, head_dim)
        ends = table[4 * g : 5 * g]
        after = jnp.sum(
            jnp.where((ends[:, None] < ends[None, :])[:, :, None], last[None], 0.0), axis=1
        )
        total = jnp.sum(jnp.exp(after)[decays_at][:, :, None, None] * states, axis=0)

    keep = jnp.exp(jnp.sum(last, axis=0))
    later = lambda by: (lambda a, b: (a + by * g, b) if a + by * g < n else None)
    if ng == 2:
        entering = exchange(total, lambda a, b: (a ^ g, b))
    else:
        entering = exchange(total, later(1))
    step = 1
    if ng > 2:
        keep = exchange(keep, later(1))
    while step < ng - 1:
        entering = entering + keep[:, None, None] * exchange(entering, later(step))
        keep = keep * exchange(keep, later(step))
        step *= 2

    normed = mix(
        tables[2], queries, keys, values, cumul, states, entering, gain, heads, head_dim
    ).reshape(g * rows, width)
    sides = [normed] + [exchange(normed, lambda a, b: (a, b ^ p)) for p in range(1, nh)]

    out_cols = model // nh
    parts = 2 if cube else 1
    if cube:
        by_plane = spread(w_out, 0, 0, plane)
        by_plane = lax.optimization_barrier((by_plane, total))[0]
        by_plane = by_plane.reshape(plane, levels, width, -1)
        local = by_plane.transpose(1, 2, 0, 3).reshape(levels, width, -1)
        cut = local.shape[-1] // parts
        cuts = lax.optimization_barrier(
            [local[:, :, i * cut : (i + 1) * cut] for i in range(parts)]
        )
        swap = (c // plane) % 2 == 1
        mine = []
        for x in cuts:
            pieces = over_planes(x)
            mine.append([])
            for p in range(nh):
                side = h ^ p ^ group
                first = jnp.where(side == 0, pieces[0], pieces[2])
                second = jnp.where(side == 0, pieces[1], pieces[3])
                ordered = [jnp.where(swap, second, first), jnp.where(swap, first, second)]
                mine[-1].append(jnp.concatenate(ordered, axis=1))
    else:
        local = spread(w_out.reshape(g, width, -1), 0, 0, g)
        local = local.transpose(1, 0, 2).reshape(width, -1)
        whole = jnp.concatenate(true_order(over_groups(local), group), axis=1)
        whole = whole.reshape(width, nh, out_cols).transpose(1, 0, 2)
        mine = [[lax.dynamic_index_in_dim(whole, h ^ p, 0, False) for p in range(nh)]]

    done = []
    for columns in mine:
        right = columns[:1] + [
            exchange(m, lambda a, b: (a, b ^ (p + 1)))
            for p, m in enumerate(columns[1:])
        ]
        partial = sum(
            jnp.dot(t, w, preferred_element_type=F32) for t, w in zip(sides, right)
        ).astype(BF16)
        chunks = max(len(bits), 1)
        span = partial.shape[1] // chunks
        summed = []
        for j in range(chunks):
            piece = partial[:, j * span : (j + 1) * span].reshape((2,) * len(bits) + (rows, -1))
            left = list(axes)
            for stage, bit in enumerate(bits[j:] + bits[:j]):
                axis = left.index(bit)
                left.pop(axis)
                kept = lax.index_in_dim(piece, 0, axis, False)
                sent = lax.index_in_dim(piece, 1, axis, False)
                got = exchange(sent, lambda a, b: (a ^ bit, b))
                piece = (kept.astype(F32) + got.astype(F32)).astype(BF16)
            summed.append(piece)
        done.append(jnp.concatenate(summed, axis=1))
    if cube:
        done = [d[:, i * cut : (i + 1) * cut] for i in range(2) for d in done]
    return jnp.concatenate(done, axis=1)


def solution(mesh):
    placed = (
        P("ctx", None),
        P("ctx", "head"),
        P("ctx", "head"),
        P("ctx", "head"),
        P("head", "ctx"),
        P("head"),
        P("head", "ctx"),
    )
    body = functools.partial(per_device, n=mesh.shape["ctx"], nh=mesh.shape["head"])

    return jax.shard_map(
        body, mesh=mesh, in_specs=placed, out_specs=P("ctx", "head"), check_vma=False
    )
```
